32 devices in a mesh: groups: 2 (over y), blk: 4 (over z), tok: 4 (over x, core).
Axes of the slice: x: 2, y: 2, z: 4, core: 2. Of those that a mesh axis runs over, the one named last changes fastest.
Arguments:
- inputs: bfloat16 [12288, 2048], P(('groups', 'tok'), 'blk'), parts along dimension 0, may hold values from -6 to 6
- targets: bfloat16 [12288, 2048], P(('groups', 'tok'), 'blk'), parts along dimension 0, may hold values from -6 to 6
- left_factor: bfloat16 [16, 256, 256], P(('groups', 'blk')), parts along dimension 0, may hold values from -0.375 to 0.375
- right_factor: bfloat16 [16, 256, 256], P(('groups', 'blk')), parts along dimension 0, may hold values from -0.375 to 0.375
Outputs:
- grad_left: float32 [16, 256, 256], P(('groups', 'blk'), 'tok'), parts along dimension 0
- grad_right: float32 [16, 256, 256], P(('groups', 'blk'), 'tok'), parts along dimension 0
The draws below stay inside these ranges and needn't reach their ends.
There are 2 independent parts, one for each index of `groups`. The reference program is written for one: setup_inputs(seed, part) draws one part's arguments, and reference() takes and returns one part's arrays. A program takes and returns all parts, laid end to end along the dimension named above; each array names one. Nothing has to cross between parts.
All inputs are finite; a program needn't handle non-finite values.
Results may differ from the reference program's by a relative error of at most 0.0015.
Values may be sent and summed in bfloat16 or wider, within the bound.
No kernel may reach another device: no remote copies, remote signals or barrier semaphores. Data moves between devices by JAX's collectives and lax.ppermute only.
A program may use at most 64 MiB of HBM per device.

```python
import jax
import jax.numpy as jnp

BS = 256
TOK_DEV = 1536
NB = 8
M = 32
D = 2048
TOKENS = 6144


def block_scale(stream_key, shape, pieces, smallest, top_value):
    level, own = 1.0, jax.random.fold_in(stream_key, 6)
    for dim, shards_of in pieces:
        steps = jnp.exp(jax.random.uniform(jax.random.fold_in(own, dim), (shards_of,), jnp.float32, smallest / len(pieces), top_value / len(pieces)))
        level = level * jnp.repeat(steps, shape[dim] // shards_of).reshape([-1 if axis == dim else 1 for axis in range(len(shape))])
    return level


def scatter_about(own_key, shape, width, most, pieces=(), kind=jnp.bfloat16):
    loudness = block_scale(own_key, shape, pieces, -0.22, 0.18) if pieces else 1.0
    values = jax.random.normal(own_key, shape, jnp.float32) * width * loudness
    return jnp.minimum(jnp.maximum(values, -most), most).astype(kind)


def setup_inputs(seed: int = 0, part: int = 0) -> dict:
    splits = jax.random.split(jax.random.key(seed), 5)
    part_splits = jax.random.split(jax.random.fold_in(splits[4], part), 5)
    inputs = scatter_about(part_splits[0], (TOKENS, D), 1.0, 6.0, ((0, 4), (1, 4)))
    targets = scatter_about(part_splits[1], (TOKENS, D), 1.0, 6.0, ((0, 4), (1, 4)))
    left_factor = scatter_about(part_splits[2], (NB, BS, BS), BS ** -0.5, 0.375, ((0, 4),))
    right_factor = scatter_about(part_splits[3], (NB, BS, BS), BS ** -0.5, 0.375, ((0, 4),))
    return dict(inputs=inputs, targets=targets, left_factor=left_factor, right_factor=right_factor)


def reference(inputs, targets, left_factor, right_factor):
    shaped = inputs.reshape(TOKENS, NB, BS)
    first_out = jnp.einsum('tki,kji->tkj', shaped.astype(jnp.float32), left_factor.astype(jnp.float32)).astype(jnp.bfloat16)
    mixed_in = first_out.reshape(TOKENS, NB, NB, M).transpose(0, 2, 1, 3).reshape(TOKENS, NB, BS)
    student = jnp.einsum('tgc,goc->tgo', mixed_in.astype(jnp.float32), right_factor.astype(jnp.float32))
    truth = targets.reshape(TOKENS, NB, BS).astype(jnp.float32)
    error_rows = (student - truth).astype(jnp.bfloat16)
    back_mixed = jnp.einsum('tgo,goc->tgc', error_rows.astype(jnp.float32), right_factor.astype(jnp.float32)).astype(jnp.bfloat16)
    back_first = back_mixed.reshape(TOKENS, NB, NB, M).transpose(0, 2, 1, 3).reshape(TOKENS, NB, BS)
    inverse_rows = jnp.float32(1.0 / TOK_DEV)
    grad_right = jnp.einsum('tgo,tgc->goc', error_rows.astype(jnp.float32), mixed_in.astype(jnp.float32)) * inverse_rows
    grad_left = jnp.einsum('tkj,tki->kji', back_first.astype(jnp.float32), shaped.astype(jnp.float32)) * inverse_rows
    return grad_left, grad_right
```

```python
import functools

import jax
import jax.numpy as jnp
from jax import lax
from jax.experimental import pallas as pl
from jax.experimental.pallas import tpu as pltpu
from jax.sharding import PartitionSpec as P

F32, BF16 = jnp.float32, jnp.bfloat16
NT = (((1,), (1,)), ((), ()))
NN = (((1,), (0,)), ((), ()))
TN = (((0,), (0,)), ((), ()))


def dot(a, b, dims):
    return lax.dot_general(a, b, dims, preferred_element_type=F32)


def after(value, *others):
    return lax.optimization_barrier((value, others))[0]


def params():
    return pltpu.CompilerParams(vmem_limit_bytes=48 << 20)


def whole(shape):
    return pl.BlockSpec(shape, lambda i: (0,) * len(shape))


def forward_kernel(peers, left_ref, x_ref, *refs):
    outs, left_rel = refs[:peers], refs[peers]
    blocks, width = left_ref.shape[0], left_ref.shape[1]
    rows = width // peers
    step = rows // blocks
    me = lax.axis_index("blk")

    @pl.when(pl.program_id(0) == 0)
    def _():
        for d in range(peers):
            at = pl.multiple_of((me ^ d) * rows, rows)
            for k in range(blocks):
                left_rel[k, d * rows : (d + 1) * rows, :] = left_ref[k, pl.ds(at, rows), :]

    for k in range(blocks):
        first = dot(left_rel[k], x_ref[:, k * width : (k + 1) * width], NT).astype(BF16)
        for d in range(peers):
            for g in range(blocks):
                low = d * rows + g * step
                outs[d][g, k * step : (k + 1) * step, :] = first[low : low + step]


def forward(left, x, peers, start, size, tile):
    blocks, width, _ = left.shape
    rows = width // peers
    base = start // tile
    return pl.pallas_call(
        functools.partial(forward_kernel, peers),
        grid=(size // tile,),
        in_specs=[
            whole(left.shape),
            pl.BlockSpec((tile, x.shape[1]), lambda i: (base + i, 0)),
        ],
        out_specs=[pl.BlockSpec((blocks, rows, tile), lambda i: (0, 0, i))] * peers,
        out_shape=[jax.ShapeDtypeStruct((blocks, rows, size), BF16)] * peers,
        scratch_shapes=[pltpu.VMEM(left.shape, BF16)],
        compiler_params=params(),
        name="forward",
    )(left, x)


def middle_kernel(peers, toks, has_prior, last, right_ref, targets_ref, *refs):
    pieces = refs[:peers]
    refs = refs[peers:]
    prior = refs[0] if has_prior else None
    refs = refs[1:] if has_prior else refs
    backs = refs[:peers]
    if last:
        terms, mixed, back, total = refs[peers : peers + toks], *refs[peers + toks :]
    else:
        total, mixed, back = refs[peers:]
    blocks, width = right_ref.shape[0], right_ref.shape[1]
    rows = width // peers
    step = rows // blocks
    me = lax.axis_index("blk")
    i = pl.program_id(0)

    @pl.when(i == 0)
    def _():
        total[...] = prior[...] if has_prior else jnp.zeros_like(total)

    for d in range(peers):
        at = pl.multiple_of((me ^ d) * rows, rows)
        for g in range(blocks):
            mixed[g, pl.ds(at, rows), :] = pieces[d][g]
    for g in range(blocks):
        truth = targets_ref[:, g * width : (g + 1) * width].astype(F32).T
        error = (dot(right_ref[g], mixed[g], NN) - truth).astype(BF16)
        back[g] = dot(right_ref[g], error, TN).astype(BF16)
        total[g] += dot(error, mixed[g], NT)
    own = lax.axis_index("tok")
    for s in range(peers):
        at = pl.multiple_of((own ^ s) * rows, rows)
        for g in range(blocks):
            part = back[g, pl.ds(at, rows), :]
            for k in range(blocks):
                backs[s][k, g * step : (g + 1) * step, :] = part[k * step : (k + 1) * step]
    if last:

        @pl.when(i == pl.num_programs(0) - 1)
        def _():
            size = width // toks
            for s in range(toks):
                at = pl.multiple_of((own ^ s) * size, size)
                terms[s][...] = total[:, pl.ds(at, size), :]


def middle(right, targets, pieces, prior, peers, toks, start, size, tile, last):
    blocks, width, _ = right.shape
    rows = width // peers
    base = start // tile
    piece = pl.BlockSpec((blocks, rows, tile), lambda i: (0, 0, i))
    grad = (blocks, width, width)
    term = (blocks, width // toks, width)
    extra = [] if prior is None else [prior]
    tail = [term] * toks if last else [grad]
    scratch = [pltpu.VMEM((blocks, width, tile), BF16)] * 2
    if last:
        scratch = scratch + [pltpu.VMEM(grad, F32)]
    return pl.pallas_call(
        functools.partial(middle_kernel, peers, toks, prior is not None, last),
        grid=(size // tile,),
        in_specs=[
            whole(right.shape),
            pl.BlockSpec((tile, targets.shape[1]), lambda i: (base + i, 0)),
        ]
        + [piece] * peers
        + [whole(grad)] * len(extra),
        out_specs=[piece] * peers + [whole(t) for t in tail],
        out_shape=[jax.ShapeDtypeStruct((blocks, rows, size), BF16)] * peers
        + [jax.ShapeDtypeStruct(t, F32) for t in tail],
        scratch_shapes=scratch,
        compiler_params=params(),
        name="middle",
    )(right, targets, *pieces, *extra)


def left_kernel(toks, scale, has_prior, *refs):
    pieces = refs[:toks]
    rows_ref = refs[toks]
    prior = refs[toks + 1] if has_prior else None
    out = refs[-1]
    blocks = out.shape[0]
    width = out.shape[2]
    mine = lax.axis_index("blk") ^ lax.axis_index("tok")

    def slot(r):
        at, bit = 0, 1
        while bit < toks:
            at = 2 * at + (r // bit) % 2
            bit *= 2
        return at

    for k in range(blocks):
        total = prior[k] if has_prior else None
        for s in range(toks):
            rows = rows_ref[slot(mine ^ s), :, k * width : (k + 1) * width]
            term = dot(pieces[s][k], rows, NN)
            total = term if total is None else total + term
        out[k] = total * scale


def left_rows(pieces, gathered, prior, toks, scale, start, size, width):
    blocks, rows, _ = pieces[0].shape
    shape = (blocks, rows, width)
    extra = [] if prior is None else [prior]
    at = start // size
    return pl.pallas_call(
        functools.partial(left_kernel, toks, scale, prior is not None),
        grid=(1,),
        in_specs=[whole(pieces[0].shape)] * toks
        + [pl.BlockSpec((toks, size, gathered.shape[2]), lambda i: (0, at, 0))]
        + [whole(shape)] * len(extra),
        out_specs=whole(shape),
        out_shape=jax.ShapeDtypeStruct(shape, F32),
        compiler_params=params(),
        name="left_rows",
    )(*pieces, gathered, *extra)


def on_device(inputs, targets, left_factor, right_factor):
    width = left_factor.shape[1]
    tok_rows = inputs.shape[0]
    peers = lax.axis_size("blk")
    toks = lax.axis_size("tok")
    inverse_rows = 1.0 / tok_rows
    chunks = ((0, tok_rows * 2 // 3), (tok_rows * 2 // 3, tok_rows // 3))
    tile = tok_rows // 3

    def over(axis, size, d):
        return functools.partial(
            lax.ppermute, axis_name=axis, perm=[(j, j ^ d) for j in range(size)]
        )

    def homeward(s):
        pairs = [
            (b * toks + t, (t ^ s) * toks + b) for b in range(peers) for t in range(toks)
        ]
        return functools.partial(lax.ppermute, axis_name=("blk", "tok"), perm=pairs)

    arrived = []
    left = left_factor
    for start, size in chunks:
        pieces = forward(left, inputs, peers, start, size, tile)
        left = after(left_factor, *pieces)
        order = sorted(range(1, peers), reverse=True)
        got = {d: over("blk", peers, d)(pieces[d]) for d in order}
        arrived.append([pieces[0]] + [got[d] for d in range(1, peers)])

    gathered = after(inputs, *pieces)[None]
    hop = toks // 2
    crossed = over("tok", toks, hop)(gathered)

    prior, sent = None, []
    for c, (start, size) in enumerate(chunks):
        last = c == len(chunks) - 1
        res = middle(
            right_factor, targets, arrived[c], prior, peers, toks, start, size, tile, last
        )
        backs, rest = res[:peers], res[peers:]
        prior = rest[0]
        sent.append(backs)
    terms = rest

    home = [[homeward(s)(backs[s]) for s in range(toks)] for backs in sent]
    while hop:
        gathered = jnp.concatenate([gathered, after(crossed, *terms)])
        hop //= 2
        if hop:
            crossed = over("tok", toks, hop)(gathered)

    terms = after(tuple(terms), home[0][0])
    summed_right = terms[0]
    for s in range(1, toks):
        summed_right = summed_right + over("tok", toks, s)(terms[s])

    total = None
    for c, (start, size) in enumerate(chunks):
        scale = inverse_rows if c == len(chunks) - 1 else 1.0
        total = left_rows(home[c], gathered, total, toks, scale, start, size, width)
    return (total, summed_right * jnp.float32(inverse_rows))


def solution(mesh):
    in_specs = (
        P(("groups", "tok"), "blk"),
        P(("groups", "tok"), "blk"),
        P(("groups", "blk"), None, None),
        P(("groups", "blk"), None, None),
    )
    out_specs = (P(("groups", "blk"), "tok", None), P(("groups", "blk"), "tok", None))
    return jax.shard_map(
        on_device, mesh=mesh, in_specs=in_specs, out_specs=out_specs, check_vma=False
    )
```

```python
import functools

import jax
import jax.numpy as jnp
from jax import lax
from jax.experimental import pallas as pl
from jax.experimental.pallas import tpu as pltpu
from jax.sharding import PartitionSpec as P

F32, BF16 = jnp.float32, jnp.bfloat16
NT = (((1,), (1,)), ((), ()))
NN = (((1,), (0,)), ((), ()))
TN = (((0,), (0,)), ((), ()))


def dot(a, b, dims):
    return lax.dot_general(a, b, dims, preferred_element_type=F32)


def after(value, *others):
    return lax.optimization_barrier((value, others))[0]


def call(kernel, name, flops, **kwargs):
    moved = sum(
        s.size * s.dtype.itemsize for s in jax.tree.leaves(kwargs["out_shape"])
    )
    return pl.pallas_call(
        kernel,
        name=name,
        compiler_params=pltpu.CompilerParams(vmem_limit_bytes=24 << 20),
        cost_estimate=pl.CostEstimate(flops=flops, bytes_accessed=2 * moved, transcendentals=0),
        **kwargs,
    )


def whole(shape):
    return pl.BlockSpec(shape, lambda i: (0,) * len(shape))


def forward_kernel(peers, g, left_ref, x_ref, *refs):
    outs, held = refs[:peers], refs[peers]
    blocks, width = left_ref.shape[0], left_ref.shape[1]
    rows = width // peers
    step = rows // blocks
    me = lax.axis_index("blk")

    @pl.when(pl.program_id(0) == 0)
    def _():
        for d in range(peers):
            at = pl.multiple_of((me ^ d) * rows + g * step, step)
            for k in range(blocks):
                held[k, d * step : (d + 1) * step, :] = left_ref[k, pl.ds(at, step), :]

    for k in range(blocks):
        first = dot(held[k], x_ref[:, k * width : (k + 1) * width], NT).astype(BF16)
        for d in range(peers):
            outs[d][k] = first[d * step : (d + 1) * step]


def forward(left, x, peers, g, tile):
    blocks, width, _ = left.shape
    step = width // peers // blocks
    tokens = x.shape[0]
    return call(
        functools.partial(forward_kernel, peers, g),
        "forward",
        2 * tokens * width * width,
        grid=(tokens // tile,),
        in_specs=[whole(left.shape), pl.BlockSpec((tile, x.shape[1]), lambda i: (i, 0))],
        out_specs=[pl.BlockSpec((blocks, step, tile), lambda i: (0, 0, i))] * peers,
        out_shape=[jax.ShapeDtypeStruct((blocks, step, tokens), BF16)] * peers,
        scratch_shapes=[pltpu.VMEM((blocks, peers * step, width), BF16)],
    )(left, x)


def middle_kernel(peers, toks, g, right_ref, targets_ref, *refs):
    pieces, backs, terms = refs[:peers], refs[peers : 2 * peers], refs[2 * peers : 2 * peers + toks]
    mixed, back, total = refs[2 * peers + toks :]
    blocks, step, _ = pieces[0].shape
    width = right_ref.shape[1]
    rows = blocks * step
    me, own = lax.axis_index("blk"), lax.axis_index("tok")
    i = pl.program_id(0)

    @pl.when(i == 0)
    def _():
        total[...] = jnp.zeros_like(total)

    for d in range(peers):
        for k in range(blocks):
            at = pl.multiple_of((me ^ d) * rows + k * step, step)
            mixed[pl.ds(at, step), :] = pieces[d][k]
    error = (dot(right_ref[g], mixed[...], NN) - targets_ref[...].astype(F32).T).astype(BF16)
    back[...] = dot(right_ref[g], error, TN).astype(BF16)
    for d in range(peers):
        for k in range(blocks):
            at = pl.multiple_of((me ^ d) * rows + k * step, step)
            backs[d][k] = back[pl.ds(at, step), :]
    total[...] += dot(error, mixed[...], NT)

    @pl.when(i == pl.num_programs(0) - 1)
    def _():
        size = width // toks
        for s in range(toks):
            at = pl.multiple_of((own ^ s) * size, size)
            terms[s][...] = total[pl.ds(at, size), :]


def middle(right, targets, pieces, toks, g, tile):
    peers = len(pieces)
    blocks, step, tokens = pieces[0].shape
    width = right.shape[1]
    piece = pl.BlockSpec((blocks, step, tile), lambda i: (0, 0, i))
    term = (width // toks, width)
    return call(
        functools.partial(middle_kernel, peers, toks, g),
        "middle",
        6 * tokens * width * width,
        grid=(tokens // tile,),
        in_specs=[whole(right.shape), pl.BlockSpec((tile, width), lambda i: (i, g))]
        + [piece] * peers,
        out_specs=[piece] * peers + [whole(term)] * toks,
        out_shape=[jax.ShapeDtypeStruct(pieces[0].shape, BF16)] * peers
        + [jax.ShapeDtypeStruct(term, F32)] * toks,
        scratch_shapes=[
            pltpu.VMEM((width, tile), BF16),
            pltpu.VMEM((width, tile), BF16),
            pltpu.VMEM((width, width), F32),
        ],
    )(right, targets, *pieces)


def left_kernel(peers, toks, carried, x_ref, *refs):
    pieces, refs = refs[:peers], refs[peers:]
    extras, outs, (joined, partial) = refs[: carried * toks], refs[carried * toks : -2], refs[-2:]
    blocks, step, _ = pieces[0].shape
    width = x_ref.shape[1] // blocks
    mine = lax.axis_index("blk") ^ lax.axis_index("tok")
    for k in range(blocks):
        for d in range(peers):
            joined[d * step : (d + 1) * step, :] = pieces[d][k]
        partial[k] = dot(joined[...], x_ref[:, k * width : (k + 1) * width], NN)
    for s in range(toks):
        at = pl.multiple_of((mine ^ s) * step, step)
        for k in range(blocks):
            outs[s][carried, k * step : (k + 1) * step, :] = partial[k, pl.ds(at, step), :]
        for n in range(carried):
            outs[s][n] = extras[n * toks + s][...]


def left_terms(x, pieces, extras, toks):
    peers = len(pieces)
    blocks, step, tokens = pieces[0].shape
    width = x.shape[1] // blocks
    carried = len(extras)
    flat = [e[s] for e in extras for s in range(toks)]
    return call(
        functools.partial(left_kernel, peers, toks, carried),
        "left_terms",
        2 * tokens * width * width,
        in_specs=[pl.BlockSpec(memory_space=pltpu.VMEM)] * (1 + peers + len(flat)),
        out_specs=[pl.BlockSpec(memory_space=pltpu.VMEM)] * toks,
        out_shape=[jax.ShapeDtypeStruct((carried + 1, blocks * step, width), F32)] * toks,
        scratch_shapes=[
            pltpu.VMEM((peers * step, tokens), BF16),
            pltpu.VMEM((blocks, peers * step, width), F32),
        ],
    )(x, *pieces, *flat)


def finish_kernel(toks, groups, scale, *refs):
    sums = refs[: toks * groups]
    left_out, right_out = refs[toks * groups :]
    blocks, rows, _ = left_out.shape
    step = rows // groups
    for g in range(groups):
        parts = sums[g * toks : (g + 1) * toks]
        last = parts[0].shape[0] - 1
        total = parts[0][last]
        for p in parts[1:]:
            total = total + p[last]
        total = total * scale
        for k in range(blocks):
            left_out[k, g * step : (g + 1) * step, :] = total[k * step : (k + 1) * step]
        if last:
            for n in range(last):
                total = parts[0][n]
                for p in parts[1:]:
                    total = total + p[n]
                right_out[n] = total * scale


def finish(groups, blocks, scale):
    toks = len(groups[0])
    _, rows, width = groups[0][0].shape
    flat = [a for group in groups for a in group]
    shape = jax.ShapeDtypeStruct((blocks, rows, width), F32)
    return call(
        functools.partial(finish_kernel, toks, len(groups), scale),
        "finish",
        1,
        in_specs=[pl.BlockSpec(memory_space=pltpu.VMEM)] * len(flat),
        out_specs=[pl.BlockSpec(memory_space=pltpu.VMEM)] * 2,
        out_shape=[shape] * 2,
    )(*flat)


def on_device(inputs, targets, left_factor, right_factor):
    tokens = inputs.shape[0]
    blocks = left_factor.shape[0]
    peers = lax.axis_size("blk")
    toks = lax.axis_size("tok")
    tile = tokens // 3

    def swap(axis, size, d, value):
        return lax.ppermute(value, axis, [(j, j ^ d) for j in range(size)])

    def exchange(axis, pieces):
        size = len(pieces)
        got = {d: swap(axis, size, d, pieces[d]) for d in range(size - 1, 0, -1)}
        return [pieces[0]] + [got[d] for d in range(1, size)]

    left, arrived = left_factor, []
    for g in range(blocks):
        sent = forward(left, inputs, peers, g, tile)
        left = after(left_factor, *sent)
        arrived.append(exchange("blk", sent))

    right, returned, terms = right_factor, [], []
    for g in range(blocks):
        res = middle(right, targets, arrived[g], toks, g, tile)
        right = after(right_factor, *res[:peers])
        returned.append(exchange("blk", res[:peers]))
        terms.append(res[peers:])

    rows, sums = inputs, []
    for g in range(blocks):
        out = left_terms(rows, returned[g], terms if g == 0 else [], toks)
        rows = after(inputs, *out)
        sums.append(exchange("tok", out))
    return tuple(finish(sums, blocks, 1.0 / tokens))


def solution(mesh):
    in_specs = (
        P(("groups", "tok"), "blk"),
        P(("groups", "tok"), "blk"),
        P(("groups", "blk"), None, None),
        P(("groups", "blk"), None, None),
    )
    out_specs = (P(("groups", "blk"), "tok", None), P(("groups", "blk"), "tok", None))
    return jax.shard_map(
        on_device, mesh=mesh, in_specs=in_specs, out_specs=out_specs, check_vma=False
    )
```

```python
import functools

import jax
import jax.numpy as jnp
from jax import lax
from jax.experimental import pallas as pl
from jax.experimental.pallas import tpu as pltpu
from jax.sharding import PartitionSpec as P

F32, BF16 = jnp.float32, jnp.bfloat16
ORDERS = ((2, 3, 1), (1, 2, 3)), ((2, 3, 1), (1, 2, 3))
NT = (((1,), (1,)), ((), ()))
NN = (((1,), (0,)), ((), ()))
TN = (((0,), (0,)), ((), ()))


def dot(a, b, dims):
    return lax.dot_general(a, b, dims, preferred_element_type=F32)


def after(value, *others):
    return lax.optimization_barrier((value, others))[0]


def listed(kind, peers, g):
    first = [d for d in ORDERS[kind][g % 2] if d < peers]
    return first + [d for d in range(peers) if d not in first]


def call(kernel, name, flops, **kwargs):
    moved = sum(
        s.size * s.dtype.itemsize for s in jax.tree.leaves(kwargs["out_shape"])
    )
    return pl.pallas_call(
        kernel,
        name=name,
        compiler_params=pltpu.CompilerParams(vmem_limit_bytes=24 << 20),
        cost_estimate=pl.CostEstimate(flops=flops, bytes_accessed=2 * moved, transcendentals=0),
        **kwargs,
    )


def in_hbm(value):
    return pltpu.with_memory_space_constraint(value, pltpu.HBM)


def whole(shape):
    return pl.BlockSpec(shape, lambda i: (0,) * len(shape))


def forward_kernel(peers, g, tiles, left_ref, x_ref, *refs):
    outs, (held, whole_left, rows_in, left_sem, row_sems) = refs[:peers], refs[peers:]
    blocks, width = left_ref.shape[0], left_ref.shape[1]
    rows = width // peers
    step = rows // blocks
    tile = x_ref.shape[0] // tiles
    me = lax.axis_index("blk")
    fetch = pltpu.make_async_copy(left_ref, whole_left, left_sem)
    fetch.start()
    loads = []
    for n in range(tiles):
        at = pl.ds(n * tile, tile)
        loads.append(pltpu.make_async_copy(x_ref.at[at], rows_in.at[at], row_sems.at[n]))
        loads[-1].start()
    fetch.wait()
    for d in range(peers):
        at = pl.multiple_of((me ^ d) * rows + g * step, step)
        for k in range(blocks):
            held[k, d * step : (d + 1) * step, :] = whole_left[k, pl.ds(at, step), :]
    for n in range(tiles):
        loads[n].wait()
        low = n * tile
        for k in range(blocks):
            part = rows_in[low : low + tile, k * width : (k + 1) * width]
            first = dot(held[k], part, NT).astype(BF16)
            for d in range(peers):
                outs[d][k, :, low : low + tile] = first[d * step : (d + 1) * step]


def forward(left, x, peers, g, tiles):
    blocks, width, _ = left.shape
    step = width // peers // blocks
    tokens = x.shape[0]
    return call(
        functools.partial(forward_kernel, peers, g, tiles),
        "forward",
        2 * tokens * width * width,
        in_specs=[pl.BlockSpec(memory_space=pltpu.HBM)] * 2,
        out_specs=[pl.BlockSpec(memory_space=pltpu.VMEM)] * peers,
        out_shape=[jax.ShapeDtypeStruct((blocks, step, tokens), BF16)] * peers,
        scratch_shapes=[
            pltpu.VMEM((blocks, peers * step, width), BF16),
            pltpu.VMEM(left.shape, BF16),
            pltpu.VMEM(x.shape, BF16),
            pltpu.SemaphoreType.DMA,
            pltpu.SemaphoreType.DMA((tiles,)),
        ],
    )(in_hbm(left), in_hbm(x))


def middle_kernel(peers, toks, g, order, right_ref, targets_ref, *refs):
    pieces, backs, terms = refs[:peers], refs[peers : 2 * peers], refs[2 * peers : 2 * peers + toks]
    pieces = [pieces[order.index(d)] for d in range(peers)]
    mixed, back, total = refs[2 * peers + toks :]
    blocks, step, _ = pieces[0].shape
    width = right_ref.shape[1]
    rows = blocks * step
    me, own = lax.axis_index("blk"), lax.axis_index("tok")
    i = pl.program_id(0)

    @pl.when(i == 0)
    def _():
        total[...] = jnp.zeros_like(total)

    for d in range(peers):
        for k in range(blocks):
            at = pl.multiple_of((me ^ d) * rows + k * step, step)
            mixed[pl.ds(at, step), :] = pieces[d][k]
    error = (dot(right_ref[g], mixed[...], NN) - targets_ref[...].astype(F32).T).astype(BF16)
    back[...] = dot(right_ref[g], error, TN).astype(BF16)
    for d in range(peers):
        for k in range(blocks):
            at = pl.multiple_of((me ^ d) * rows + k * step, step)
            backs[d][k] = back[pl.ds(at, step), :]
    total[...] += dot(error, mixed[...], NT)

    @pl.when(i == pl.num_programs(0) - 1)
    def _():
        size = width // toks
        for s in range(toks):
            at = pl.multiple_of((own ^ s) * size, size)
            terms[s][...] = total[pl.ds(at, size), :]


def middle(right, targets, pieces, toks, g, tile):
    peers = len(pieces)
    order = listed(0, peers, g)
    blocks, step, tokens = pieces[0].shape
    width = right.shape[1]
    piece = pl.BlockSpec((blocks, step, tile), lambda i: (0, 0, i))
    term = (width // toks, width)
    return call(
        functools.partial(middle_kernel, peers, toks, g, order),
        "middle",
        6 * tokens * width * width,
        grid=(tokens // tile,),
        in_specs=[whole(right.shape), pl.BlockSpec((tile, width), lambda i: (i, g))]
        + [piece] * peers,
        out_specs=[piece] * peers + [whole(term)] * toks,
        out_shape=[jax.ShapeDtypeStruct(pieces[0].shape, BF16)] * peers
        + [jax.ShapeDtypeStruct(term, F32)] * toks,
        scratch_shapes=[
            pltpu.VMEM((width, tile), BF16),
            pltpu.VMEM((width, tile), BF16),
            pltpu.VMEM((width, width), F32),
        ],
    )(right, in_hbm(targets), *[pieces[d] for d in order])


def left_kernel(peers, toks, carried, order, x_ref, *refs):
    pieces, refs = [refs[order.index(d)] for d in range(peers)], refs[peers:]
    extras, outs, (joined, partial) = refs[: carried * toks], refs[carried * toks : -2], refs[-2:]
    blocks, step, _ = pieces[0].shape
    width = x_ref.shape[1] // blocks
    parts = len(outs)
    mine = lax.axis_index("blk") ^ lax.axis_index("tok")
    for k in range(blocks):
        for d in range(peers):
            joined[d * step : (d + 1) * step, :] = pieces[d][k]
        partial[k] = dot(joined[...], x_ref[:, k * width : (k + 1) * width], NN)
    for s in range(toks):
        at = pl.multiple_of((mine ^ s) * step, step)
        for k in range(blocks):
            outs[s % parts][s // parts, carried, k * step : (k + 1) * step, :] = partial[k, pl.ds(at, step), :]
        for n in range(carried):
            outs[s % parts][s // parts, n] = extras[n * toks + s][...]


def left_terms(x, pieces, extras, toks, parts, g):
    peers = len(pieces)
    order = listed(1, peers, g)
    blocks, step, tokens = pieces[0].shape
    width = x.shape[1] // blocks
    carried = len(extras)
    flat = [e[s] for e in extras for s in range(toks)]
    return call(
        functools.partial(left_kernel, peers, toks, carried, order),
        "left_terms",
        2 * tokens * width * width,
        in_specs=[pl.BlockSpec(memory_space=pltpu.VMEM)] * (1 + peers + len(flat)),
        out_specs=[pl.BlockSpec(memory_space=pltpu.VMEM)] * parts,
        out_shape=[jax.ShapeDtypeStruct((toks // parts, carried + 1, blocks * step, width), F32)]
        * parts,
        scratch_shapes=[
            pltpu.VMEM((peers * step, tokens), BF16),
            pltpu.VMEM((blocks, peers * step, width), F32),
        ],
    )(x, *[pieces[d] for d in order], *flat)


def fold_kernel(keep_ref, got_ref, keep_out, send_out):
    for n in range(keep_ref.shape[0]):
        (send_out if n % 2 else keep_out)[n // 2] = keep_ref[n] + got_ref[n]


def fold(keep, got):
    half = jax.ShapeDtypeStruct((keep.shape[0] // 2,) + keep.shape[1:], F32)
    return call(
        fold_kernel,
        "fold",
        1,
        in_specs=[pl.BlockSpec(memory_space=pltpu.VMEM)] * 2,
        out_specs=[pl.BlockSpec(memory_space=pltpu.VMEM)] * 2,
        out_shape=[half] * 2,
    )(keep, got)


def finish_kernel(counts, scale, *refs):
    left_out, right_out = refs[sum(counts) :]
    blocks, rows, _ = left_out.shape
    step = rows // len(counts)
    for g, count in enumerate(counts):
        parts, refs = refs[:count], refs[count:]
        last = parts[0].shape[1] - 1
        for n in range(last + 1):
            total = parts[0][0, n]
            for p in parts[1:]:
                total = total + p[0, n]
            total = total * scale
            if n < last:
                right_out[n] = total
            else:
                for k in range(blocks):
                    left_out[k, g * step : (g + 1) * step, :] = total[k * step : (k + 1) * step]


def finish(groups, blocks, scale):
    _, _, rows, width = groups[0][0].shape
    flat = [a for group in groups for a in group]
    shape = jax.ShapeDtypeStruct((blocks, rows, width), F32)
    return call(
        functools.partial(finish_kernel, [len(group) for group in groups], scale),
        "finish",
        1,
        in_specs=[pl.BlockSpec(memory_space=pltpu.VMEM)] * len(flat),
        out_specs=[pl.BlockSpec(memory_space=pltpu.VMEM)] * 2,
        out_shape=[shape] * 2,
    )(*flat)


def on_device(inputs, targets, left_factor, right_factor):
    tokens = inputs.shape[0]
    blocks = left_factor.shape[0]
    peers = lax.axis_size("blk")
    toks = lax.axis_size("tok")
    tile = tokens // 3

    def swap(axis, size, d, value):
        return lax.ppermute(value, axis, [(j, j ^ d) for j in range(size)])

    def exchange(axis, pieces):
        size = len(pieces)
        got = {d: swap(axis, size, d, pieces[d]) for d in range(size - 1, 0, -1)}
        return [pieces[0]] + [got[d] for d in range(1, size)]

    left, arrived = left_factor, []
    for g in range(blocks):
        sent = forward(left, inputs, peers, g, 2)
        left = after(left_factor, *sent)
        arrived.append(exchange("blk", sent))

    right, returned, terms = right_factor, [], []
    for g in range(blocks):
        res = middle(right, targets, arrived[g], toks, g, tile)
        right = after(right_factor, *res[:peers])
        returned.append(exchange("blk", res[:peers]))
        terms.append(res[peers:])

    rows, groups = inputs, []
    for g in range(blocks):
        last = g == blocks - 1
        extras = terms if g == 0 else []
        out = left_terms(rows, returned[g], extras, toks, 2 if last else toks, g)
        rows = after(inputs, *out)
        if last:
            keep, send = out
            got, hop = swap("tok", toks, 1, send), 2
            got = after(got, *groups[0]) if toks > 2 else got
            while hop < toks:
                keep, send = fold(keep, got)
                got, hop = swap("tok", toks, hop, send), 2 * hop
            groups.append([keep, got])
        else:
            groups.append(exchange("tok", out))
    return tuple(finish(groups, blocks, 1.0 / tokens))


def solution(mesh):
    in_specs = (
        P(("groups", "tok"), "blk"),
        P(("groups", "tok"), "blk"),
        P(("groups", "blk"), None, None),
        P(("groups", "blk"), None, None),
    )
    out_specs = (P(("groups", "blk"), "tok", None), P(("groups", "blk"), "tok", None))
    return jax.shard_map(
        on_device, mesh=mesh, in_specs=in_specs, out_specs=out_specs, check_vma=False
    )
```

```python
import functools

import jax
import jax.numpy as jnp
from jax import lax
from jax.experimental import pallas as pl
from jax.experimental.pallas import tpu as pltpu
from jax.sharding import PartitionSpec as P

F32, BF16 = jnp.float32, jnp.bfloat16
ORDERS = ((2, 3, 1), (1, 2, 3)), ((2, 3, 1), (1, 2, 3))
NT = (((1,), (1,)), ((), ()))
NN = (((1,), (0,)), ((), ()))
TN = (((0,), (0,)), ((), ()))


def dot(a, b, dims):
    return lax.dot_general(a, b, dims, preferred_element_type=F32)


def after(value, *others):
    return lax.optimization_barrier((value, others))[0]


def listed(kind, peers, g):
    first = [d for d in ORDERS[kind][g % 2] if d < peers]
    return first + [d for d in range(peers) if d not in first]


def call(kernel, name, flops, **kwargs):
    moved = sum(
        s.size * s.dtype.itemsize for s in jax.tree.leaves(kwargs["out_shape"])
    )
    return pl.pallas_call(
        kernel,
        name=name,
        compiler_params=pltpu.CompilerParams(vmem_limit_bytes=24 << 20),
        cost_estimate=pl.CostEstimate(flops=flops, bytes_accessed=2 * moved, transcendentals=0),
        **kwargs,
    )


def in_hbm(value):
    return pltpu.with_memory_space_constraint(value, pltpu.HBM)


def whole(shape):
    return pl.BlockSpec(shape, lambda i: (0,) * len(shape))


def forward_kernel(peers, g, tiles, left_ref, x_ref, *refs):
    outs, (held, whole_left, rows_in, left_sem, row_sems) = refs[:peers], refs[peers:]
    blocks, width = left_ref.shape[0], left_ref.shape[1]
    rows = width // peers
    step = rows // blocks
    tokens = x_ref.shape[0]
    marks = [0, tokens // 3, tokens]
    me = lax.axis_index("blk")
    fetch = pltpu.make_async_copy(left_ref, whole_left, left_sem)
    fetch.start()
    loads = []
    for n in range(tiles):
        at = pl.ds(marks[n], marks[n + 1] - marks[n])
        loads.append(pltpu.make_async_copy(x_ref.at[at], rows_in.at[at], row_sems.at[n]))
        loads[-1].start()
    fetch.wait()
    for d in range(peers):
        at = pl.multiple_of((me ^ d) * rows + g * step, step)
        for k in range(blocks):
            held[k, d * step : (d + 1) * step, :] = whole_left[k, pl.ds(at, step), :]
    for n in range(tiles):
        loads[n].wait()
        low, high = marks[n], marks[n + 1]
        for k in range(blocks):
            part = rows_in[low:high, k * width : (k + 1) * width]
            first = dot(held[k], part, NT).astype(BF16)
            for d in range(peers):
                outs[d][k, :, low:high] = first[d * step : (d + 1) * step]


def forward(left, x, peers, g, tiles):
    blocks, width, _ = left.shape
    step = width // peers // blocks
    tokens = x.shape[0]
    return call(
        functools.partial(forward_kernel, peers, g, tiles),
        "forward",
        2 * tokens * width * width,
        in_specs=[pl.BlockSpec(memory_space=pltpu.HBM)] * 2,
        out_specs=[pl.BlockSpec(memory_space=pltpu.VMEM)] * peers,
        out_shape=[jax.ShapeDtypeStruct((blocks, step, tokens), BF16)] * peers,
        scratch_shapes=[
            pltpu.VMEM((blocks, peers * step, width), BF16),
            pltpu.VMEM(left.shape, BF16),
            pltpu.VMEM(x.shape, BF16),
            pltpu.SemaphoreType.DMA,
            pltpu.SemaphoreType.DMA((tiles,)),
        ],
    )(in_hbm(left), in_hbm(x))


def middle_kernel(peers, toks, g, order, right_ref, targets_ref, *refs):
    pieces, backs, terms = refs[:peers], refs[peers : 2 * peers], refs[2 * peers : 2 * peers + toks]
    pieces = [pieces[order.index(d)] for d in range(peers)]
    mixed, back, total = refs[2 * peers + toks :]
    blocks, step, _ = pieces[0].shape
    width = right_ref.shape[1]
    rows = blocks * step
    me, own = lax.axis_index("blk"), lax.axis_index("tok")
    i = pl.program_id(0)

    @pl.when(i == 0)
    def _():
        total[...] = jnp.zeros_like(total)

    for d in range(peers):
        for k in range(blocks):
            at = pl.multiple_of((me ^ d) * rows + k * step, step)
            mixed[pl.ds(at, step), :] = pieces[d][k]
    error = (dot(right_ref[g], mixed[...], NN) - targets_ref[...].astype(F32).T).astype(BF16)
    back[...] = dot(right_ref[g], error, TN).astype(BF16)
    for d in range(peers):
        for k in range(blocks):
            at = pl.multiple_of((me ^ d) * rows + k * step, step)
            backs[d][k] = back[pl.ds(at, step), :]
    total[...] += dot(error, mixed[...], NT)

    @pl.when(i == pl.num_programs(0) - 1)
    def _():
        size = width // toks
        for s in range(toks):
            at = pl.multiple_of((own ^ s) * size, size)
            terms[s][...] = total[pl.ds(at, size), :]


def middle(right, targets, pieces, toks, g, tile):
    peers = len(pieces)
    order = listed(0, peers, g)
    blocks, step, tokens = pieces[0].shape
    width = right.shape[1]
    piece = pl.BlockSpec((blocks, step, tile), lambda i: (0, 0, i))
    term = (width // toks, width)
    return call(
        functools.partial(middle_kernel, peers, toks, g, order),
        "middle",
        6 * tokens * width * width,
        grid=(tokens // tile,),
        in_specs=[whole(right.shape), pl.BlockSpec((tile, width), lambda i: (i, g))]
        + [piece] * peers,
        out_specs=[piece] * peers + [whole(term)] * toks,
        out_shape=[jax.ShapeDtypeStruct(pieces[0].shape, BF16)] * peers
        + [jax.ShapeDtypeStruct(term, F32)] * toks,
        scratch_shapes=[
            pltpu.VMEM((width, tile), BF16),
            pltpu.VMEM((width, tile), BF16),
            pltpu.VMEM((width, width), F32),
        ],
    )(right, in_hbm(targets), *[pieces[d] for d in order])


def left_kernel(peers, toks, carried, order, x_ref, *refs):
    pieces, refs = [refs[order.index(d)] for d in range(peers)], refs[peers:]
    extras, outs, (joined, partial) = refs[: carried * toks], refs[carried * toks : -2], refs[-2:]
    blocks, step, _ = pieces[0].shape
    width = x_ref.shape[1] // blocks
    parts = len(outs)
    mine = lax.axis_index("blk") ^ lax.axis_index("tok")
    for k in range(blocks):
        for d in range(peers):
            joined[d * step : (d + 1) * step, :] = pieces[d][k]
        partial[k] = dot(joined[...], x_ref[:, k * width : (k + 1) * width], NN)
    for s in range(toks):
        at = pl.multiple_of((mine ^ s) * step, step)
        for k in range(blocks):
            outs[s % parts][s // parts, carried, k * step : (k + 1) * step, :] = partial[k, pl.ds(at, step), :]
        for n in range(carried):
            outs[s % parts][s // parts, n] = extras[n * toks + s][...]


def left_terms(x, pieces, extras, toks, parts, g):
    peers = len(pieces)
    order = listed(1, peers, g)
    blocks, step, tokens = pieces[0].shape
    width = x.shape[1] // blocks
    carried = len(extras)
    flat = [e[s] for e in extras for s in range(toks)]
    return call(
        functools.partial(left_kernel, peers, toks, carried, order),
        "left_terms",
        2 * tokens * width * width,
        in_specs=[pl.BlockSpec(memory_space=pltpu.VMEM)] * (1 + peers + len(flat)),
        out_specs=[pl.BlockSpec(memory_space=pltpu.VMEM)] * parts,
        out_shape=[jax.ShapeDtypeStruct((toks // parts, carried + 1, blocks * step, width), F32)]
        * parts,
        scratch_shapes=[
            pltpu.VMEM((peers * step, tokens), BF16),
            pltpu.VMEM((blocks, peers * step, width), F32),
        ],
    )(x, *[pieces[d] for d in order], *flat)


def fold_kernel(keep_ref, got_ref, keep_out, send_out):
    for n in range(keep_ref.shape[0]):
        (send_out if n % 2 else keep_out)[n // 2] = keep_ref[n] + got_ref[n]


def fold(keep, got):
    half = jax.ShapeDtypeStruct((keep.shape[0] // 2,) + keep.shape[1:], F32)
    return call(
        fold_kernel,
        "fold",
        1,
        in_specs=[pl.BlockSpec(memory_space=pltpu.VMEM)] * 2,
        out_specs=[pl.BlockSpec(memory_space=pltpu.VMEM)] * 2,
        out_shape=[half] * 2,
    )(keep, got)


def sum_kernel(count, scale, *refs):
    parts, (rows_out, *right_out) = refs[:count], refs[count:]
    last = parts[0].shape[1] - 1
    for n in range(last + 1):
        total = parts[0][0, n]
        for p in parts[1:]:
            total = total + p[0, n]
        if n < last:
            right_out[0][n] = total * scale
        else:
            rows_out[...] = total * scale


def tok_sum(group, scale):
    _, height, rows, width = group[0].shape
    shapes = [jax.ShapeDtypeStruct((rows, width), F32)]
    if height > 1:
        shapes.append(jax.ShapeDtypeStruct((height - 1, rows, width), F32))
    return call(
        functools.partial(sum_kernel, len(group), scale),
        "tok_sum",
        1,
        in_specs=[pl.BlockSpec(memory_space=pltpu.VMEM)] * len(group),
        out_specs=[pl.BlockSpec(memory_space=pltpu.VMEM)] * len(shapes),
        out_shape=shapes,
    )(*group)


def finish_kernel(scale, keep, got, *refs):
    done, left_out = refs[:-1], refs[-1]
    blocks, rows, _ = left_out.shape
    step = rows // (len(done) + 1)
    total = (keep[0, 0] + got[0, 0]) * scale
    for k in range(blocks):
        for g, ref in enumerate(done):
            left_out[k, g * step : (g + 1) * step, :] = ref[k * step : (k + 1) * step, :]
        left_out[k, rows - step :, :] = total[k * step : (k + 1) * step]


def finish(keep, got, done, blocks, scale):
    _, _, rows, width = keep.shape
    return call(
        functools.partial(finish_kernel, scale),
        "finish",
        1,
        in_specs=[pl.BlockSpec(memory_space=pltpu.VMEM)] * (2 + len(done)),
        out_specs=pl.BlockSpec(memory_space=pltpu.VMEM),
        out_shape=jax.ShapeDtypeStruct((blocks, rows, width), F32),
    )(keep, got, *done)


def on_device(inputs, targets, left_factor, right_factor):
    tokens = inputs.shape[0]
    blocks = left_factor.shape[0]
    peers = lax.axis_size("blk")
    toks = lax.axis_size("tok")
    tile = tokens // 2

    def swap(axis, size, d, value):
        return lax.ppermute(value, axis, [(j, j ^ d) for j in range(size)])

    def exchange(axis, pieces):
        size = len(pieces)
        got = {d: swap(axis, size, d, pieces[d]) for d in range(size - 1, 0, -1)}
        return [pieces[0]] + [got[d] for d in range(1, size)]

    left, arrived = left_factor, []
    for g in range(blocks):
        sent = forward(left, inputs, peers, g, 2)
        left = after(left_factor, *sent)
        arrived.append(exchange("blk", sent))

    right, returned, terms = right_factor, [], []
    for g in range(blocks):
        res = middle(right, targets, arrived[g], toks, g, tile)
        right = after(right_factor, *res[:peers])
        sent = list(res[:peers])
        if g:
            sent[-1] = after(sent[-1], returned[0][-1])
        returned.append(exchange("blk", sent))
        terms.append(res[peers:])

    rows, groups = inputs, []
    for g in range(blocks):
        last = g == blocks - 1
        extras = terms if g == 0 else []
        out = left_terms(rows, returned[g], extras, toks, 2 if last else toks, g)
        rows = after(inputs, *out)
        if last:
            keep, send = out
            got, hop = swap("tok", toks, 1, send), 2
            got = after(got, *groups[0]) if toks > 2 else got
            while hop < toks:
                keep, send = fold(keep, got)
                got, hop = swap("tok", toks, hop, send), 2 * hop
        else:
            groups.append(exchange("tok", out))
    scale = 1.0 / tokens
    done, grad_right = [], None
    for group in groups:
        rows, *right = tok_sum(group, scale)
        done.append(rows)
        grad_right = right[0] if right else grad_right
    return finish(keep, got, done, blocks, scale), grad_right


def solution(mesh):
    in_specs = (
        P(("groups", "tok"), "blk"),
        P(("groups", "tok"), "blk"),
        P(("groups", "blk"), None, None),
        P(("groups", "blk"), None, None),
    )
    out_specs = (P(("groups", "blk"), "tok", None), P(("groups", "blk"), "tok", None))
    return jax.shard_map(
        on_device, mesh=mesh, in_specs=in_specs, out_specs=out_specs, check_vma=False
    )
```
